32 devices in a mesh: group: 1, ctx: 32 (over z, y, x, core).
Axes of the slice: x: 2, y: 2, z: 4, core: 2. Of those that a mesh axis runs over, the one named last changes fastest.
Arguments:
- queries: bfloat16 [2, 64, 128], P('group'), may hold values from -80 to 80
- key_cache: bfloat16 [2, 4096, 512], P('group', 'ctx'), may hold values from -4 to 4
- value_cache: bfloat16 [2, 4096, 512], P('group', 'ctx'), may hold values from -6 to 6
- out_weight: bfloat16 [8192, 4096], P('ctx'), may hold values from -0.125 to 0.125
- hidden_in: bfloat16 [2, 4096], P('group'), may hold values from -45 to 45
- norm_gain: float32 [4096], replicated, may hold values from 0.25 to 1.75
- gate_weight: bfloat16 [32, 4096, 192], P('ctx'), may hold values from -0.09375 to 0.09375
- up_weight: bfloat16 [32, 4096, 192], P('ctx'), may hold values from -0.09375 to 0.09375
- down_weight: bfloat16 [32, 192, 4096], P('ctx'), may hold values from -0.15625 to 0.15625
- routes: int32 [2, 4], P('group'), may hold values from 0 to 3, all different within a row; in each aligned block of 2 rows (0 to 1, 2 to 3, ...) at most 2 rows name the same one
- route_weight: float32 [2, 4], P('group'), may hold values from 0.1 to 1
Outputs:
- mixed: float32 [2, 4096], P('group', 'ctx')
The draws below stay inside these ranges and needn't reach their ends.
Inputs may be any that keep to these rules, and one draw needn't show every extreme that they name: `routes`: each row names 4 different experts; no expert is named by more than 2 rows, a bound that some block reaches.
All inputs are finite; a program needn't handle non-finite values.
Results may differ from the reference program's by a relative error of at most 0.0035.
Values may be sent and summed in bfloat16 or wider, within the bound.
A program may use at most 64 MiB of HBM per device.

```python
import math
import jax
import jax.numpy as jnp
import numpy as np
from jax import lax

D = 4096
HEADS = 64
KVH = 4
HD = 128
FF = 1536
QUARTERS = 8
TOP = 4
SEQS = 2
CONTEXT = 4096
EXPERTS = 4
SHARDS = 32
HID_DEV = 192
CAP = 2


def attention_pair(key):
    base_key = jax.random.fold_in(key, 17)
    key_q, key_k = jax.random.split(base_key, 2)
    key_vals = jnp.clip(jax.random.normal(key_k, (SEQS, CONTEXT, KVH, HD), jnp.float32), -4.0, 4.0)
    query_vals = jnp.clip(2.5 * jax.random.normal(key_q, (SEQS, HEADS, HD), jnp.float32), -10.0, 10.0)
    return (query_vals, key_vals.reshape(SEQS, CONTEXT, KVH * HD))


def draw_queries(key, part):
    return attention_pair(key)[0].astype(jnp.bfloat16)


def draw_key_cache(key, part):
    return attention_pair(key)[1].astype(jnp.bfloat16)


def draw_hidden_in(key, part):
    key_a = jax.random.fold_in(jax.random.fold_in(key, 29), 0)
    column = jnp.arange(D, dtype=jnp.float32) / D
    values = jnp.clip(jax.random.normal(key_a, (SEQS, D), jnp.float32), -4.0, 4.0) * jnp.power(3.0, column)[None, :] / math.sqrt(3.0)
    return values.astype(jnp.bfloat16)


def strengthened(drawn, rng, source, target, parts, factor):
    owner, partner = [(jnp.arange(drawn.shape[position]) // (drawn.shape[position] // parts)).reshape([-1 if axis == position else 1 for axis in range(drawn.ndim)]) for position in (source, target)]
    chosen = jax.random.permutation(rng, parts)[partner]
    strong = (owner == chosen) | (owner == (partner + parts // 2) % parts)
    return jnp.where(strong, factor * drawn, drawn)


def steps_of(key, shape, shards, smallest, largest):
    def one(position, blocks):
        heights = jax.random.uniform(jax.random.fold_in(jax.random.fold_in(key, 6), position), (blocks,), jnp.float32, smallest / len(shards), largest / len(shards))
        return jnp.repeat(jnp.exp(heights), shape[position] // blocks).reshape((-1,) + (1,) * (len(shape) - position - 1))

    factor_of = one(*shards[0])
    for cut in shards[1:]:
        factor_of = factor_of * one(*cut)
    return factor_of


def shared_out(stream_key, own, number, rows, count, top, most, slope):
    ranking = jax.random.permutation(stream_key, count)
    heavy_load, usual = load_shares(count, rows * top, most, slope, True), load_shares(count, rows * top, most, slope, False)
    places = jnp.arange(count)

    def named(tallies, turn):
        used = int((tallies > 0).sum())
        fixed = max(1, used // 4)
        shifted = fixed + (places - fixed + turn * (used - fixed)) % max(1, count - fixed)
        return jnp.zeros((count,), jnp.int32).at[ranking[jnp.where(places < fixed, places, shifted)]].set(jnp.asarray(tallies, jnp.int32))

    tallies = jnp.where(number % 4 == 0, named(heavy_load, number // 4), named(usual, number - number // 4 - 1))
    mixed = jax.random.permutation(jax.random.fold_in(own, 3), count)
    source_of, sink = mixed[0:count // 2 * 2:2], mixed[1:count // 2 * 2:2]
    margin = jnp.minimum(tallies[source_of] - 1, most - tallies[sink]) // 2
    margin = jnp.where((source_of == ranking[0]) | (sink == ranking[0]) | (tallies[sink] == 0), 0, jnp.maximum(margin, 0))
    shifted = jax.random.randint(jax.random.fold_in(own, 4), (count // 2,), 0, 1 << 20) % (margin + 1)
    tallies = tallies.at[source_of].add(-shifted).at[sink].add(shifted)
    items = jnp.searchsorted(jnp.cumsum(tallies), jnp.arange(rows * top), side="right").astype(jnp.int32)
    table = items.reshape(top, rows).T
    table = table[jax.random.permutation(jax.random.fold_in(own, 1), rows)]
    turn = jax.random.randint(jax.random.fold_in(own, 2), (rows, 1), 0, top)
    return jnp.take_along_axis(table, (jnp.arange(top)[None, :] + turn) % top, axis=1)


def load_shares(amount, total, limit, lean, full):
    weights = [(1 << 20) // math.isqrt(standing ** lean) + 1 for standing in range(1, amount + 1)]
    largest = limit if full else min(limit, max(-(-total // amount), total * weights[0] // sum(weights)))
    least = 1 if total - largest >= amount - 1 else 0
    counts, spare = [largest] + [least] * (amount - 1), total - largest - least * (amount - 1)
    while spare > 0:
        free = [i for i in range(1, amount) if counts[i] < largest] or [i for i in range(1, amount) if counts[i] < limit]
        mass, left = sum([weights[i] for i in free]), spare
        for i in free:
            addition = min(limit - counts[i], max(1, left * weights[i] // mass), spare)
            counts[i] = counts[i] + addition
            spare = spare - addition
    return np.array(counts)


def noise(rng, dims, width, limit, cuts=(), kind=jnp.bfloat16):
    values = jax.random.normal(rng, dims, jnp.float32) * width
    if len(cuts) > 0:
        values = steps_of(rng, dims, cuts, -0.22, 0.18) * values
    return jnp.clip(values, min=-limit, max=limit).astype(kind)


def heavy_noise(stream_key, dims, deviation, most, shards, heavy, kind=jnp.bfloat16):
    result = deviation * jax.random.normal(stream_key, dims, jnp.float32)
    if shards:
        result = result * steps_of(stream_key, dims, shards, -0.22, 0.18)
    return jnp.clip(strengthened(result, jax.random.fold_in(stream_key, 3), *heavy), -most, most).astype(kind)


def setup_inputs(seed: int = 0, part: int = 0) -> dict:
    splits = jax.random.split(jax.random.key(seed), 12)
    part_splits = jax.random.split(jax.random.fold_in(splits[11], part), 12)
    queries = draw_queries(jax.random.fold_in(jax.random.fold_in(splits[11], part), 71), part)
    key_cache = draw_key_cache(jax.random.fold_in(jax.random.fold_in(splits[11], part), 71), part)
    value_cache = noise(part_splits[2], (SEQS, CONTEXT, KVH * HD), 1.0, 6.0, ((1, 32),))
    out_weight = heavy_noise(splits[3], (HEADS * HD, D), (HEADS * HD) ** -0.5, 0.125, ((0, 32),), (0, 1, 32, 2.75))
    hidden_in = draw_hidden_in(jax.random.fold_in(jax.random.fold_in(splits[11], part), 71), part)
    norm_gain = jnp.clip(1.0 + 0.15 * jax.random.normal(splits[5], (D,), jnp.float32), 0.25, 1.75)
    gate_weight = noise(splits[6], (SHARDS, D, HID_DEV), D ** -0.5, 0.09375, ((0, 32),))
    up_weight = noise(splits[7], (SHARDS, D, HID_DEV), D ** -0.5, 0.09375, ((0, 32),))
    down_weight = noise(splits[8], (SHARDS, HID_DEV, D), FF ** -0.5, 0.15625, ((0, 32),))
    routes_keys = jax.random.split(jax.random.fold_in(part_splits[9], 1), SEQS // SEQS)
    routes_turns = jax.random.permutation(jax.random.fold_in(part_splits[9], 3), SEQS // SEQS)
    routes = jax.vmap(lambda own, number: shared_out(jax.random.fold_in(part_splits[9], 2), own, number, SEQS, EXPERTS, TOP, CAP, 2))(routes_keys, routes_turns).reshape((SEQS, TOP))
    route_weight = jnp.clip(jax.random.uniform(part_splits[10], (SEQS, TOP), jnp.float32, 0.1, 1.0), 0.1, 1.0)
    return {"queries": queries, "key_cache": key_cache, "value_cache": value_cache, "out_weight": out_weight, "hidden_in": hidden_in, "norm_gain": norm_gain, "gate_weight": gate_weight, "up_weight": up_weight, "down_weight": down_weight, "routes": routes, "route_weight": route_weight}


def slot_numbers(routes, expert_count):
    flat_routes = routes.reshape(-1)
    onehot = (flat_routes[:, None] == jnp.arange(expert_count, dtype=jnp.int32)[None, :]).astype(jnp.int32)
    before = jnp.cumsum(onehot, axis=0) - onehot
    return lax.optimization_barrier(jnp.sum(before * onehot, axis=1)).astype(jnp.int32)

def reference(queries, key_cache, value_cache, out_weight, hidden_in, norm_gain, gate_weight, up_weight, down_weight, routes, route_weight):
    group_size = HEADS // KVH
    query_view = queries.reshape(SEQS, KVH, group_size, HD).astype(jnp.float32)
    key_view = key_cache.reshape(SEQS, CONTEXT, KVH, HD).astype(jnp.float32)
    value_view = value_cache.reshape(SEQS, CONTEXT, KVH, HD).astype(jnp.float32)
    scores = jnp.einsum('sgjd,scgd->sgjc', query_view, key_view) * HD ** (-0.5)
    row_peak = lax.optimization_barrier(jnp.max(scores, axis=-1, keepdims=True))
    numer = jnp.exp(scores - row_peak)
    denoms = lax.optimization_barrier(jnp.sum(numer, axis=-1))
    probs = lax.optimization_barrier(numer.astype(jnp.bfloat16)).astype(jnp.float32)
    weighted = jnp.einsum('sgjc,scgd->sgjd', probs, value_view)
    attended = (weighted / denoms[..., None]).reshape(SEQS, HEADS * HD).astype(jnp.bfloat16)
    projected = jnp.dot(attended, out_weight, preferred_element_type=jnp.float32)
    resid = hidden_in.astype(jnp.float32) + projected
    inverse_rms = lax.rsqrt(lax.optimization_barrier(jnp.mean(resid * resid, axis=-1, keepdims=True)) + 1e-06)
    normed = (resid * inverse_rms * norm_gain.astype(jnp.float32)).astype(jnp.bfloat16)
    slot_index = slot_numbers(routes, EXPERTS)
    flat_routes = routes.reshape(-1)
    token_of = jnp.arange(SEQS * TOP, dtype=jnp.int32) // TOP
    weight_flat = route_weight.reshape(-1).astype(jnp.float32)
    slot_range = jnp.arange(CAP, dtype=jnp.int32)

    def one_shard(shard_args):
        shard_index, gate_part, up_part, down_part = shard_args
        expert = shard_index // QUARTERS
        matches = (flat_routes[None, :] == expert) & (slot_index[None, :] == slot_range[:, None])
        slot_token = lax.optimization_barrier(jnp.sum(matches.astype(jnp.int32) * token_of[None, :], axis=1)).astype(jnp.int32)
        slot_weight = lax.optimization_barrier(jnp.sum(matches.astype(jnp.float32) * weight_flat[None, :], axis=1))
        picked_rows = normed[slot_token]
        gate_act = jnp.dot(picked_rows, gate_part, preferred_element_type=jnp.float32)
        up_act = jnp.dot(picked_rows, up_part, preferred_element_type=jnp.float32)
        hidden = (jax.nn.silu(gate_act) * up_act).astype(jnp.bfloat16)
        return jnp.dot(hidden, down_part, preferred_element_type=jnp.float32) * slot_weight[:, None]
    expert_out = lax.map(one_shard, (jnp.arange(SHARDS, dtype=jnp.int32), gate_weight, up_weight, down_weight))
    grouped = expert_out.reshape(EXPERTS, QUARTERS, CAP, D)
    gathered = grouped[routes, :, slot_index.reshape(SEQS, TOP)]
    moe = lax.optimization_barrier(jnp.sum(gathered, axis=(1, 2)))
    return resid + moe
```

```python
import functools

import jax
import jax.numpy as jnp
from jax import lax
from jax.experimental import pallas as pl
from jax.experimental.pallas import tpu as pltpu
from jax.sharding import PartitionSpec as P

QUARTERS = 8
LANES = 128
eps = 1e-06
MESH = pl.DeviceIdType.MESH


def kernel(
    n,
    queries,
    key_cache,
    value_cache,
    out_weight,
    hidden_in,
    gain,
    gate_weight,
    up_weight,
    down_weight,
    routes,
    route_weight,
    out,
    q_v,
    k_v,
    v_v,
    ow_v,
    hid_v,
    gain_v,
    gate_v,
    up_v,
    down_v,
    routes_v,
    rw_v,
    send_a,
    recv_a,
    att_v,
    send_b,
    recv_b,
    full_v,
    xn_v,
    send_c,
    recv_c,
    load_sem,
    send_sem,
    recv_sem,
):
    me = lax.axis_index("ctx")
    seqs, heads, head_dim = q_v.shape
    kv_heads = k_v.shape[2] // head_dim
    per_kv = heads // kv_heads
    width = hid_v.shape[1]
    feat_rows = out_weight.shape[0]
    feat_ratio = ow_v.shape[0] // feat_rows
    groups = send_a.shape[0]
    hpd = heads // groups
    rows = seqs * hpd
    blocks, _, block = send_b.shape
    block_ratio = n // blocks
    my_block = me // block_ratio

    loads = []
    pairs = (
        [(queries, q_v), (key_cache, k_v), (value_cache, v_v)]
        + [
            (out_weight, ow_v.at[pl.ds(j * feat_rows, feat_rows)] if feat_ratio > 1 else ow_v)
            for j in range(feat_ratio)
        ]
        + [(hidden_in, hid_v), (gain, gain_v)]
        + [(gate_weight.at[0], gate_v), (up_weight.at[0], up_v), (down_weight.at[0], down_v)]
        + [(routes, routes_v), (route_weight, rw_v)]
    )
    for i, (src, dst) in enumerate(pairs):
        copy = pltpu.make_async_copy(src, dst, load_sem.at[i])
        copy.start()
        loads.append(copy)

    barrier = pltpu.get_barrier_semaphore()

    def greet(o, carry):
        pl.semaphore_signal(
            barrier, inc=1, device_id={"ctx": lax.rem(me + o, n)}, device_id_type=MESH
        )
        return carry

    lax.fori_loop(1, n, greet, 0)

    def send_all(phase, source, target):
        def one(o, carry):
            peer = lax.rem(me + o, n)
            pltpu.make_async_remote_copy(
                src_ref=source(peer),
                dst_ref=target(o),
                send_sem=send_sem.at[phase],
                recv_sem=recv_sem.at[phase],
                device_id={"ctx": peer},
                device_id_type=MESH,
            ).start()
            return carry

        lax.fori_loop(1, n, one, 0)

    def arrived(phase, ref):
        whole = ref.at[pl.ds(1, n - 1)]
        return pltpu.make_async_remote_copy(
            src_ref=whole,
            dst_ref=whole,
            send_sem=send_sem.at[phase],
            recv_sem=recv_sem.at[phase],
            device_id={"ctx": me},
            device_id_type=MESH,
        )

    for i in range(3):
        loads[i].wait()
    scale = head_dim ** (-0.5)
    low_half = lax.broadcasted_iota(jnp.int32, (per_kv, head_dim), 1) < head_dim // 2
    for s in range(seqs):
        for g in range(kv_heads):
            scores = (
                lax.dot_general(
                    q_v[s, g * per_kv : (g + 1) * per_kv, :],
                    k_v[s, :, g * head_dim : (g + 1) * head_dim],
                    (((1,), (1,)), ((), ())),
                    preferred_element_type=jnp.float32,
                )
                * scale
            )
            peak = jnp.max(scores, axis=-1, keepdims=True)
            numer = jnp.exp(scores - peak)
            total = jnp.sum(numer, axis=-1, keepdims=True)
            weighted = jnp.dot(
                numer.astype(jnp.bfloat16),
                v_v[s, :, g * head_dim : (g + 1) * head_dim],
                preferred_element_type=jnp.float32,
            )
            stats = jnp.where(low_half, peak, total)
            for t in range(per_kv // hpd):
                at = g * (per_kv // hpd) + t
                send_a[at, s * hpd : (s + 1) * hpd, :] = weighted[t * hpd : (t + 1) * hpd]
                send_a[at, rows + s * hpd : rows + (s + 1) * hpd, :] = stats[
                    t * hpd : (t + 1) * hpd
                ]

    pl.semaphore_wait(barrier, n - 1)
    send_all(0, lambda peer: send_a.at[peer // feat_ratio], lambda o: recv_a.at[o])
    recv_a[0] = send_a[me // feat_ratio]
    for copy in loads[3:]:
        copy.wait()
    weight_of = jnp.sum(
        jnp.where(routes_v[...] == me // QUARTERS, rw_v[...], 0.0), axis=1, keepdims=True
    )
    arrived(0, recv_a).wait_recv()

    stats = recv_a[:, rows : 2 * rows, :]
    peaks = stats[:, :, 0:1]
    totals = stats[:, :, head_dim // 2 : head_dim // 2 + 1]
    factor = jnp.exp(peaks - jnp.max(peaks, axis=0, keepdims=True))
    denom = jnp.sum(factor * totals, axis=0)
    summed = jnp.sum(factor * recv_a[:, 0:rows, :], axis=0)
    attended = summed / denom
    if feat_ratio > 1:
        lane = lax.broadcasted_iota(jnp.int32, attended.shape, 1)
        attended = jnp.where(lane // feat_rows == lax.rem(me, feat_ratio), attended, 0.0)
    for s in range(seqs):
        for j in range(hpd):
            att_v[s : s + 1, j * head_dim : (j + 1) * head_dim] = attended[
                s * hpd + j : s * hpd + j + 1
            ]

    projected = jnp.dot(
        att_v[...].astype(jnp.bfloat16), ow_v[...], preferred_element_type=jnp.float32
    )
    for b in range(blocks):
        send_b[b] = projected[:, b * block : (b + 1) * block]
    send_all(1, lambda peer: send_b.at[peer // block_ratio], lambda o: recv_b.at[o])
    recv_b[0] = send_b[my_block]
    mine = hid_v[:, pl.ds(pl.multiple_of(my_block * block, block), block)].astype(jnp.float32)
    arrived(1, recv_b).wait_recv()
    resid_mine = mine + jnp.sum(recv_b[...], axis=0)
    full_v[me] = resid_mine
    send_all(2, lambda peer: full_v.at[me], lambda o: full_v.at[me])
    arrived(2, full_v).wait_recv()

    square = jnp.zeros((seqs, block), jnp.float32)
    for b in range(blocks):
        piece = full_v[b * block_ratio]
        square = square + piece * piece
    inverse = lax.rsqrt(jnp.sum(square, axis=1, keepdims=True) / width + eps)
    for b in range(blocks):
        xn_v[:, b * block : (b + 1) * block] = (
            full_v[b * block_ratio] * inverse * gain_v[b : b + 1, :]
        ).astype(jnp.bfloat16)
    normed = xn_v[...]
    gate_act = jnp.dot(normed, gate_v[...], preferred_element_type=jnp.float32)
    up_act = jnp.dot(normed, up_v[...], preferred_element_type=jnp.float32)
    hidden = (gate_act / (1.0 + jnp.exp(-gate_act)) * up_act).astype(jnp.bfloat16)
    expert_out = jnp.dot(hidden, down_v[...], preferred_element_type=jnp.float32) * weight_of
    for b in range(blocks):
        send_c[b] = expert_out[:, b * block : (b + 1) * block]
    send_all(3, lambda peer: send_c.at[peer // block_ratio], lambda o: recv_c.at[o])
    recv_c[0] = send_c[my_block]
    arrived(3, recv_c).wait_recv()
    out[...] = resid_mine + jnp.sum(recv_c[...], axis=0)
    for phase, ref in enumerate((recv_a, recv_b, full_v, recv_c)):
        arrived(phase, ref).wait_send()


def body(
    queries,
    key_cache,
    value_cache,
    out_weight,
    hidden_in,
    norm_gain,
    gate_weight,
    up_weight,
    down_weight,
    routes,
    route_weight,
):
    n = lax.axis_size("ctx")
    seqs, heads, head_dim = queries.shape
    width = hidden_in.shape[1]
    feat = max(out_weight.shape[0], head_dim)
    groups = heads * head_dim // feat
    rows = seqs * (heads // groups)
    block = max(width // n, LANES)
    blocks = width // block
    gain = norm_gain.reshape(blocks, block)
    operands = (
        queries,
        key_cache,
        value_cache,
        out_weight,
        hidden_in,
        gain,
        gate_weight,
        up_weight,
        down_weight,
        routes,
        route_weight,
    )
    f32, bf16 = jnp.float32, jnp.bfloat16
    feat_ratio = feat // out_weight.shape[0]
    result = pl.pallas_call(
        functools.partial(kernel, n),
        out_shape=jax.ShapeDtypeStruct((seqs, block), f32),
        in_specs=[pl.BlockSpec(memory_space=pl.ANY)] * len(operands),
        out_specs=pl.BlockSpec(memory_space=pltpu.VMEM),
        scratch_shapes=[
            pltpu.VMEM(queries.shape, bf16),
            pltpu.VMEM(key_cache.shape, bf16),
            pltpu.VMEM(value_cache.shape, bf16),
            pltpu.VMEM((feat, width), bf16),
            pltpu.VMEM(hidden_in.shape, bf16),
            pltpu.VMEM(gain.shape, f32),
            pltpu.VMEM(gate_weight.shape[1:], bf16),
            pltpu.VMEM(up_weight.shape[1:], bf16),
            pltpu.VMEM(down_weight.shape[1:], bf16),
            pltpu.VMEM(routes.shape, jnp.int32),
            pltpu.VMEM(route_weight.shape, f32),
            pltpu.VMEM((groups, 2 * rows, head_dim), f32),
            pltpu.VMEM((n, 2 * rows, head_dim), f32),
            pltpu.VMEM((seqs, feat), f32),
            pltpu.VMEM((blocks, seqs, block), f32),
            pltpu.VMEM((n, seqs, block), f32),
            pltpu.VMEM((n, seqs, block), f32),
            pltpu.VMEM((seqs, width), bf16),
            pltpu.VMEM((blocks, seqs, block), f32),
            pltpu.VMEM((n, seqs, block), f32),
            pltpu.SemaphoreType.DMA((len(operands) + feat_ratio - 1,)),
            pltpu.SemaphoreType.DMA((4,)),
            pltpu.SemaphoreType.DMA((4,)),
        ],
        compiler_params=pltpu.CompilerParams(
            collective_id=0, has_side_effects=True, vmem_limit_bytes=48 << 20
        ),
    )(*operands)
    col = width // n
    if col < block:
        result = lax.dynamic_slice_in_dim(
            result, lax.rem(lax.axis_index("ctx"), block // col) * col, col, 1
        )
    return result


def solution(mesh):
    in_specs = (
        P("group", None, None),
        P("group", "ctx", None),
        P("group", "ctx", None),
        P("ctx", None),
        P("group", None),
        P(),
        P("ctx", None, None),
        P("ctx", None, None),
        P("ctx", None, None),
        P("group", None),
        P("group", None),
    )
    out_specs = P("group", "ctx")
    return jax.shard_map(body, mesh=mesh, in_specs=in_specs, out_specs=out_specs, check_vma=False)
```

```python
import functools

import jax
import jax.numpy as jnp
from jax import lax
from jax.experimental import pallas as pl
from jax.experimental.pallas import tpu as pltpu
from jax.sharding import PartitionSpec as P

QUARTERS = 8
LANES = 128
eps = 1e-06
MESH = pl.DeviceIdType.MESH


def kernel(
    n,
    queries,
    key_cache,
    value_cache,
    out_weight,
    hidden_in,
    gain,
    gate_weight,
    up_weight,
    down_weight,
    routes,
    route_weight,
    out,
    q_v,
    k_v,
    v_v,
    ow_v,
    hid_v,
    gain_v,
    gate_v,
    up_v,
    down_v,
    routes_v,
    rw_v,
    send_a,
    recv_a,
    att_v,
    send_b,
    recv_b,
    full_v,
    xn_v,
    send_c,
    recv_c,
    load_sem,
    send_sem,
    recv_sem,
):
    me = lax.axis_index("ctx")
    seqs, heads, head_dim = q_v.shape
    kv_heads = k_v.shape[2] // head_dim
    per_kv = heads // kv_heads
    width = hid_v.shape[1]
    feat_rows = out_weight.shape[0]
    feat_ratio = ow_v.shape[0] // feat_rows
    groups = send_a.shape[0]
    hpd = heads // groups
    rows = seqs * hpd
    blocks, _, block = send_b.shape
    block_ratio = n // blocks
    my_block = me // block_ratio

    loads = []
    pairs = (
        [(queries, q_v), (key_cache, k_v), (value_cache, v_v)]
        + [
            (out_weight, ow_v.at[pl.ds(j * feat_rows, feat_rows)] if feat_ratio > 1 else ow_v)
            for j in range(feat_ratio)
        ]
        + [(hidden_in, hid_v), (gain, gain_v)]
        + [(gate_weight.at[0], gate_v), (up_weight.at[0], up_v), (down_weight.at[0], down_v)]
        + [(routes, routes_v), (route_weight, rw_v)]
    )
    for i, (src, dst) in enumerate(pairs):
        copy = pltpu.make_async_copy(src, dst, load_sem.at[i])
        copy.start()
        loads.append(copy)

    barrier = pltpu.get_barrier_semaphore()

    def greet(o, carry):
        pl.semaphore_signal(
            barrier, inc=1, device_id={"ctx": lax.rem(me + o, n)}, device_id_type=MESH
        )
        return carry

    lax.fori_loop(1, n, greet, 0)

    def send_all(phase, source, target):
        def one(o, carry):
            peer = lax.rem(me + o, n)
            pltpu.make_async_remote_copy(
                src_ref=source(peer),
                dst_ref=target(o),
                send_sem=send_sem.at[phase],
                recv_sem=recv_sem.at[phase],
                device_id={"ctx": peer},
                device_id_type=MESH,
            ).start()
            return carry

        lax.fori_loop(1, n, one, 0)

    def arrived(phase, ref):
        whole = ref.at[pl.ds(1, n - 1)]
        return pltpu.make_async_remote_copy(
            src_ref=whole,
            dst_ref=whole,
            send_sem=send_sem.at[phase],
            recv_sem=recv_sem.at[phase],
            device_id={"ctx": me},
            device_id_type=MESH,
        )

    for i in range(3):
        loads[i].wait()
    scale = head_dim ** (-0.5)
    low_half = lax.broadcasted_iota(jnp.int32, (per_kv, head_dim), 1) < head_dim // 2
    for s in range(seqs):
        for g in range(kv_heads):
            scores = (
                lax.dot_general(
                    q_v[s, g * per_kv : (g + 1) * per_kv, :],
                    k_v[s, :, g * head_dim : (g + 1) * head_dim],
                    (((1,), (1,)), ((), ())),
                    preferred_element_type=jnp.float32,
                )
                * scale
            )
            peak = jnp.max(scores, axis=-1, keepdims=True)
            numer = jnp.exp(scores - peak)
            total = jnp.sum(numer, axis=-1, keepdims=True)
            weighted = jnp.dot(
                numer.astype(jnp.bfloat16),
                v_v[s, :, g * head_dim : (g + 1) * head_dim],
                preferred_element_type=jnp.float32,
            )
            stats = jnp.where(low_half, peak, total)
            for t in range(per_kv // hpd):
                at = g * (per_kv // hpd) + t
                send_a[at, s * hpd : (s + 1) * hpd, :] = weighted[t * hpd : (t + 1) * hpd]
                send_a[at, rows + s * hpd : rows + (s + 1) * hpd, :] = stats[
                    t * hpd : (t + 1) * hpd
                ]

    pl.semaphore_wait(barrier, n - 1)
    send_all(0, lambda peer: send_a.at[peer // feat_ratio], lambda o: recv_a.at[o])
    recv_a[0] = send_a[me // feat_ratio]
    for copy in loads[3:]:
        copy.wait()
    weight_of = jnp.sum(
        jnp.where(routes_v[...] == me // QUARTERS, rw_v[...], 0.0), axis=1, keepdims=True
    )
    arrived(0, recv_a).wait_recv()

    stats = recv_a[:, rows : 2 * rows, :]
    peaks = stats[:, :, 0:1]
    totals = stats[:, :, head_dim // 2 : head_dim // 2 + 1]
    factor = jnp.exp(peaks - jnp.max(peaks, axis=0, keepdims=True))
    denom = jnp.sum(factor * totals, axis=0)
    summed = jnp.sum(factor * recv_a[:, 0:rows, :], axis=0)
    attended = summed / denom
    if feat_ratio > 1:
        lane = lax.broadcasted_iota(jnp.int32, attended.shape, 1)
        attended = jnp.where(lane // feat_rows == lax.rem(me, feat_ratio), attended, 0.0)
    for s in range(seqs):
        for j in range(hpd):
            att_v[s : s + 1, j * head_dim : (j + 1) * head_dim] = attended[
                s * hpd + j : s * hpd + j + 1
            ]

    projected = jnp.dot(
        att_v[...].astype(jnp.bfloat16), ow_v[...], preferred_element_type=jnp.float32
    )
    for b in range(blocks):
        send_b[b] = projected[:, b * block : (b + 1) * block]
    send_all(1, lambda peer: send_b.at[peer // block_ratio], lambda o: recv_b.at[o])
    recv_b[0] = send_b[my_block]
    mine = hid_v[:, pl.ds(pl.multiple_of(my_block * block, block), block)].astype(jnp.float32)
    arrived(1, recv_b).wait_recv()
    resid_mine = mine + jnp.sum(recv_b[...], axis=0)
    full_v[me] = resid_mine
    send_all(2, lambda peer: full_v.at[me], lambda o: full_v.at[me])
    arrived(2, full_v).wait_recv()

    square = jnp.zeros((seqs, block), jnp.float32)
    for b in range(blocks):
        piece = full_v[b * block_ratio]
        square = square + piece * piece
    inverse = lax.rsqrt(jnp.sum(square, axis=1, keepdims=True) / width + eps)
    for b in range(blocks):
        xn_v[:, b * block : (b + 1) * block] = (
            full_v[b * block_ratio] * inverse * gain_v[b : b + 1, :]
        ).astype(jnp.bfloat16)
    normed = xn_v[...]
    last = (((1,), (1,)), ((), ()))
    gate_act = lax.dot_general(normed, gate_v[...], last, preferred_element_type=jnp.float32)
    up_act = lax.dot_general(normed, up_v[...], last, preferred_element_type=jnp.float32)
    hidden = (gate_act / (1.0 + jnp.exp(-gate_act)) * up_act).astype(jnp.bfloat16)
    expert_out = jnp.dot(hidden, down_v[...], preferred_element_type=jnp.float32) * weight_of
    for b in range(blocks):
        send_c[b] = expert_out[:, b * block : (b + 1) * block]
    send_all(3, lambda peer: send_c.at[peer // block_ratio], lambda o: recv_c.at[o])
    recv_c[0] = send_c[my_block]
    arrived(3, recv_c).wait_recv()
    out[...] = resid_mine + jnp.sum(recv_c[...], axis=0)
    for phase, ref in enumerate((recv_a, recv_b, full_v, recv_c)):
        arrived(phase, ref).wait_send()


def body(
    queries,
    key_cache,
    value_cache,
    out_weight,
    hidden_in,
    norm_gain,
    gate_weight,
    up_weight,
    down_weight,
    routes,
    route_weight,
):
    n = lax.axis_size("ctx")
    seqs, heads, head_dim = queries.shape
    width = hidden_in.shape[1]
    feat = max(out_weight.shape[0], head_dim)
    groups = heads * head_dim // feat
    rows = seqs * (heads // groups)
    block = max(width // n, LANES)
    blocks = width // block
    gain = norm_gain.reshape(blocks, block)
    operands = (
        queries,
        key_cache,
        value_cache,
        out_weight,
        hidden_in,
        gain,
        jnp.swapaxes(gate_weight, 1, 2),
        jnp.swapaxes(up_weight, 1, 2),
        down_weight,
        routes,
        route_weight,
    )
    f32, bf16 = jnp.float32, jnp.bfloat16
    feat_ratio = feat // out_weight.shape[0]
    result = pl.pallas_call(
        functools.partial(kernel, n),
        out_shape=jax.ShapeDtypeStruct((seqs, block), f32),
        in_specs=[pl.BlockSpec(memory_space=pl.ANY)] * len(operands),
        out_specs=pl.BlockSpec(memory_space=pltpu.VMEM),
        scratch_shapes=[
            pltpu.VMEM(queries.shape, bf16),
            pltpu.VMEM(key_cache.shape, bf16),
            pltpu.VMEM(value_cache.shape, bf16),
            pltpu.VMEM((feat, width), bf16),
            pltpu.VMEM(hidden_in.shape, bf16),
            pltpu.VMEM(gain.shape, f32),
            pltpu.VMEM(gate_weight.shape[:0:-1], bf16),
            pltpu.VMEM(up_weight.shape[:0:-1], bf16),
            pltpu.VMEM(down_weight.shape[1:], bf16),
            pltpu.VMEM(routes.shape, jnp.int32),
            pltpu.VMEM(route_weight.shape, f32),
            pltpu.VMEM((groups, 2 * rows, head_dim), f32),
            pltpu.VMEM((n, 2 * rows, head_dim), f32),
            pltpu.VMEM((seqs, feat), f32),
            pltpu.VMEM((blocks, seqs, block), f32),
            pltpu.VMEM((n, seqs, block), f32),
            pltpu.VMEM((n, seqs, block), f32),
            pltpu.VMEM((seqs, width), bf16),
            pltpu.VMEM((blocks, seqs, block), f32),
            pltpu.VMEM((n, seqs, block), f32),
            pltpu.SemaphoreType.DMA((len(operands) + feat_ratio - 1,)),
            pltpu.SemaphoreType.DMA((4,)),
            pltpu.SemaphoreType.DMA((4,)),
        ],
        compiler_params=pltpu.CompilerParams(
            collective_id=0, has_side_effects=True
        ),
    )(*operands)
    col = width // n
    if col < block:
        result = lax.dynamic_slice_in_dim(
            result, lax.rem(lax.axis_index("ctx"), block // col) * col, col, 1
        )
    return result


def solution(mesh):
    in_specs = (
        P("group", None, None),
        P("group", "ctx", None),
        P("group", "ctx", None),
        P("ctx", None),
        P("group", None),
        P(),
        P("ctx", None, None),
        P("ctx", None, None),
        P("ctx", None, None),
        P("group", None),
        P("group", None),
    )
    out_specs = P("group", "ctx")
    return jax.shard_map(body, mesh=mesh, in_specs=in_specs, out_specs=out_specs, check_vma=False)
```

```python
import functools

import jax
import jax.numpy as jnp
from jax import lax
from jax.experimental import pallas as pl
from jax.experimental.pallas import tpu as pltpu
from jax.sharding import PartitionSpec as P

QUARTERS = 8
LANES = 128
eps = 1e-06
MESH = pl.DeviceIdType.MESH


def kernel(
    n,
    queries,
    key_cache,
    value_cache,
    out_weight,
    hidden_in,
    gain,
    gate_weight,
    up_weight,
    down_weight,
    routes,
    route_weight,
    out,
    q_v,
    k_v,
    v_v,
    ow_v,
    hid_v,
    gain_v,
    gate_v,
    up_v,
    down_v,
    routes_v,
    rw_v,
    send_a,
    recv_a,
    att_v,
    send_b,
    recv_b,
    full_v,
    xn_v,
    send_c,
    recv_c,
    load_sem,
    send_sem,
    recv_sem,
):
    me = lax.axis_index("ctx")
    group = lax.axis_index("group")
    seqs, heads, head_dim = q_v.shape
    kv_heads = k_v.shape[2] // head_dim
    per_kv = heads // kv_heads
    width = hid_v.shape[1]
    feat_rows = out_weight.shape[0]
    feat_ratio = ow_v.shape[0] // feat_rows
    groups = send_a.shape[0]
    hpd = heads // groups
    rows = seqs * hpd
    blocks, _, block = send_b.shape
    block_ratio = n // blocks

    def shared(index, ratio):
        return lax.div(index, ratio) if ratio > 1 else index

    def peer_at(o):
        if n & (n - 1) == 0:
            return jnp.bitwise_xor(me, n - o)
        peer = me + o
        return jnp.where(peer >= n, peer - n, peer)

    my_block = shared(me, block_ratio)

    barrier = pltpu.get_barrier_semaphore()

    def greet(o, carry):
        pl.semaphore_signal(
            barrier, inc=1, device_id=(group, peer_at(o)), device_id_type=MESH
        )
        return carry

    lax.fori_loop(1, n, greet, 0)

    loads = []
    pairs = (
        [(queries, q_v), (key_cache, k_v), (value_cache, v_v)]
        + [
            (out_weight, ow_v.at[pl.ds(j * feat_rows, feat_rows)] if feat_ratio > 1 else ow_v)
            for j in range(feat_ratio)
        ]
        + [(hidden_in, hid_v), (gain, gain_v)]
        + [(gate_weight.at[0], gate_v), (up_weight.at[0], up_v), (down_weight.at[0], down_v)]
        + [(routes, routes_v), (route_weight, rw_v)]
    )
    for i, (src, dst) in enumerate(pairs):
        copy = pltpu.make_async_copy(src, dst, load_sem.at[i])
        copy.start()
        loads.append(copy)

    def send_all(phase, source, target):
        def one(o, carry):
            peer = peer_at(o)
            pltpu.make_async_remote_copy(
                src_ref=source(peer),
                dst_ref=target(o),
                send_sem=send_sem.at[phase],
                recv_sem=recv_sem.at[phase],
                device_id=(group, peer),
                device_id_type=MESH,
            ).start()
            return carry

        lax.fori_loop(1, n, one, 0)

    def arrived(phase, ref):
        whole = ref.at[pl.ds(1, n - 1)]
        return pltpu.make_async_remote_copy(
            src_ref=whole,
            dst_ref=whole,
            send_sem=send_sem.at[phase],
            recv_sem=recv_sem.at[phase],
            device_id=(group, me),
            device_id_type=MESH,
        )

    for i in range(3):
        loads[i].wait()
    scale = head_dim ** (-0.5)
    low_half = lax.broadcasted_iota(jnp.int32, (per_kv, head_dim), 1) < head_dim // 2
    for s in range(seqs):
        for g in range(kv_heads):
            scores = (
                lax.dot_general(
                    q_v[s, g * per_kv : (g + 1) * per_kv, :],
                    k_v[s, :, g * head_dim : (g + 1) * head_dim],
                    (((1,), (1,)), ((), ())),
                    preferred_element_type=jnp.float32,
                )
                * scale
            )
            peak = jnp.max(scores, axis=-1, keepdims=True)
            numer = jnp.exp(scores - peak)
            total = jnp.sum(numer, axis=-1, keepdims=True)
            weighted = jnp.dot(
                numer.astype(jnp.bfloat16),
                v_v[s, :, g * head_dim : (g + 1) * head_dim],
                preferred_element_type=jnp.float32,
            )
            stats = jnp.where(low_half, peak, total)
            for t in range(per_kv // hpd):
                at = g * (per_kv // hpd) + t
                send_a[at, s * hpd : (s + 1) * hpd, :] = weighted[t * hpd : (t + 1) * hpd]
                send_a[at, rows + s * hpd : rows + (s + 1) * hpd, :] = stats[
                    t * hpd : (t + 1) * hpd
                ]

    pl.semaphore_wait(barrier, n - 1)
    send_all(0, lambda peer: send_a.at[shared(peer, feat_ratio)], lambda o: recv_a.at[o])
    recv_a[0] = send_a[shared(me, feat_ratio)]
    late = len(loads) - 7
    for copy in loads[late:late + 2] + loads[-2:]:
        copy.wait()
    weight_of = jnp.sum(
        jnp.where(routes_v[...] == me // QUARTERS, rw_v[...], 0.0), axis=1, keepdims=True
    )
    arrived(0, recv_a).wait_recv()

    stats = recv_a[:, rows : 2 * rows, :]
    peaks = stats[:, :, 0:1]
    totals = stats[:, :, head_dim // 2 : head_dim // 2 + 1]
    factor = jnp.exp(peaks - jnp.max(peaks, axis=0, keepdims=True))
    denom = jnp.sum(factor * totals, axis=0)
    summed = jnp.sum(factor * recv_a[:, 0:rows, :], axis=0)
    attended = summed / denom
    if feat_ratio > 1:
        lane = lax.broadcasted_iota(jnp.int32, attended.shape, 1)
        attended = jnp.where(lane // feat_rows == lax.rem(me, feat_ratio), attended, 0.0)
    for s in range(seqs):
        for j in range(hpd):
            att_v[s : s + 1, j * head_dim : (j + 1) * head_dim] = attended[
                s * hpd + j : s * hpd + j + 1
            ]

    for copy in loads[3:late]:
        copy.wait()
    projected = jnp.dot(
        att_v[...].astype(jnp.bfloat16), ow_v[...], preferred_element_type=jnp.float32
    )
    for b in range(blocks):
        send_b[b] = projected[:, b * block : (b + 1) * block]
    send_all(1, lambda peer: send_b.at[shared(peer, block_ratio)], lambda o: recv_b.at[o])
    recv_b[0] = send_b[my_block]
    mine = hid_v[:, pl.ds(pl.multiple_of(my_block * block, block), block)].astype(jnp.float32)
    arrived(1, recv_b).wait_recv()
    resid_mine = mine + jnp.sum(recv_b[...], axis=0)
    full_v[me] = resid_mine
    send_all(2, lambda peer: full_v.at[me], lambda o: full_v.at[me])
    arrived(2, full_v).wait_recv()

    square = jnp.zeros((seqs, block), jnp.float32)
    for b in range(blocks):
        piece = full_v[b * block_ratio]
        square = square + piece * piece
    inverse = lax.rsqrt(jnp.sum(square, axis=1, keepdims=True) / width + eps)
    for b in range(blocks):
        xn_v[:, b * block : (b + 1) * block] = (
            full_v[b * block_ratio] * inverse * gain_v[b : b + 1, :]
        ).astype(jnp.bfloat16)
    normed = xn_v[...]
    for copy in loads[late + 2 : late + 5]:
        copy.wait()
    last = (((1,), (1,)), ((), ()))
    gate_act = lax.dot_general(normed, gate_v[...], last, preferred_element_type=jnp.float32)
    up_act = lax.dot_general(normed, up_v[...], last, preferred_element_type=jnp.float32)
    hidden = (gate_act / (1.0 + jnp.exp(-gate_act)) * up_act).astype(jnp.bfloat16)
    expert_out = jnp.dot(hidden, down_v[...], preferred_element_type=jnp.float32) * weight_of
    for b in range(blocks):
        send_c[b] = expert_out[:, b * block : (b + 1) * block]
    send_all(3, lambda peer: send_c.at[shared(peer, block_ratio)], lambda o: recv_c.at[o])
    recv_c[0] = send_c[my_block]
    arrived(3, recv_c).wait_recv()
    out[...] = resid_mine + jnp.sum(recv_c[...], axis=0)
    for phase, ref in enumerate((recv_a, recv_b, full_v, recv_c)):
        arrived(phase, ref).wait_send()


def body(
    queries,
    key_cache,
    value_cache,
    out_weight,
    hidden_in,
    norm_gain,
    gate_weight,
    up_weight,
    down_weight,
    routes,
    route_weight,
):
    n = lax.axis_size("ctx")
    seqs, heads, head_dim = queries.shape
    width = hidden_in.shape[1]
    feat = max(out_weight.shape[0], head_dim)
    groups = heads * head_dim // feat
    rows = seqs * (heads // groups)
    block = max(width // n, LANES)
    blocks = width // block
    gain = norm_gain.reshape(blocks, block)
    operands = (
        queries,
        key_cache,
        value_cache,
        out_weight,
        hidden_in,
        gain,
        jnp.swapaxes(gate_weight, 1, 2),
        jnp.swapaxes(up_weight, 1, 2),
        down_weight,
        routes,
        route_weight,
    )
    f32, bf16 = jnp.float32, jnp.bfloat16
    feat_ratio = feat // out_weight.shape[0]
    result = pl.pallas_call(
        functools.partial(kernel, n),
        out_shape=jax.ShapeDtypeStruct((seqs, block), f32),
        in_specs=[pl.BlockSpec(memory_space=pl.ANY)] * len(operands),
        out_specs=pl.BlockSpec(memory_space=pltpu.VMEM),
        scratch_shapes=[
            pltpu.VMEM(queries.shape, bf16),
            pltpu.VMEM(key_cache.shape, bf16),
            pltpu.VMEM(value_cache.shape, bf16),
            pltpu.VMEM((feat, width), bf16),
            pltpu.VMEM(hidden_in.shape, bf16),
            pltpu.VMEM(gain.shape, f32),
            pltpu.VMEM(gate_weight.shape[:0:-1], bf16),
            pltpu.VMEM(up_weight.shape[:0:-1], bf16),
            pltpu.VMEM(down_weight.shape[1:], bf16),
            pltpu.VMEM(routes.shape, jnp.int32),
            pltpu.VMEM(route_weight.shape, f32),
            pltpu.VMEM((groups, 2 * rows, head_dim), f32),
            pltpu.VMEM((n, 2 * rows, head_dim), f32),
            pltpu.VMEM((seqs, feat), f32),
            pltpu.VMEM((blocks, seqs, block), f32),
            pltpu.VMEM((n, seqs, block), f32),
            pltpu.VMEM((n, seqs, block), f32),
            pltpu.VMEM((seqs, width), bf16),
            pltpu.VMEM((blocks, seqs, block), f32),
            pltpu.VMEM((n, seqs, block), f32),
            pltpu.SemaphoreType.DMA((len(operands) + feat_ratio - 1,)),
            pltpu.SemaphoreType.DMA((4,)),
            pltpu.SemaphoreType.DMA((4,)),
        ],
        compiler_params=pltpu.CompilerParams(
            collective_id=0, has_side_effects=True
        ),
    )(*operands)
    col = width // n
    if col < block:
        result = lax.dynamic_slice_in_dim(
            result, lax.rem(lax.axis_index("ctx"), block // col) * col, col, 1
        )
    return result


def solution(mesh):
    in_specs = (
        P("group", None, None),
        P("group", "ctx", None),
        P("group", "ctx", None),
        P("ctx", None),
        P("group", None),
        P(),
        P("ctx", None, None),
        P("ctx", None, None),
        P("ctx", None, None),
        P("group", None),
        P("group", None),
    )
    out_specs = P("group", "ctx")
    return jax.shard_map(body, mesh=mesh, in_specs=in_specs, out_specs=out_specs, check_vma=False)
```
